256 devices in a mesh: tm: 8 (over x, z_lo), space: 32 (over z_hi, y, core).
Axes of the slice: x: 4, y: 4, z: 8 (z_hi: 4, z_lo: 2; z = z_hi * 2 + z_lo), core: 2. Of those that a mesh axis runs over, the one named last changes fastest.
Arguments:
- panels_in: float32 [32, 16384], P(None, 'space'), may hold values from -120 to 120
- blocks: float32 [16, 256, 3, 4096], P('tm', 'space'), may hold values from -0.4375 to 0.4375
- block_mask: int32 [16, 256, 3], P('tm', 'space'), may hold values 0 or 1
- mixing: float32 [16, 4, 8, 8], P('tm'), may hold values from -0.6 to 0.6
Outputs:
- forward_states: float32 [8, 32, 16384], P('tm', None, 'space')
- adjoint_states: float32 [8, 32, 16384], P('tm', None, 'space')
The draws below stay inside these ranges and needn't reach their ends.
All inputs are finite; a program needn't handle non-finite values. No bound on the sum of `block_mask` on one device may be relied on, other than what follows from the above.
Results may differ from the reference program's by a relative error of at most 0.0003.
Values sent between devices are 32-bit elements; how exact they have to be, the bound alone decides.
A program may use at most 64 MiB of HBM per device.

```python
import jax
import jax.numpy as jnp
from jax import lax

BLOCK = 64
COLS = 8
PANELS = 4
TRANSFER_RUN = 2
STEPS = 16
NBOX = 16384
NBLK = 256
N_TM = 8


def draw_panels_in(key, part):
    subkeys = jax.random.split(key, 3)
    row_count = NBOX
    width_all = PANELS * COLS
    position = jnp.arange(row_count, dtype=jnp.float32) / row_count
    rising = jnp.exp(jnp.log(3.0) * position)
    row_scale = jnp.exp(jnp.log(10.0) * (jax.random.uniform(subkeys[0], (row_count,), jnp.float32) - 0.5))
    col_scale = jnp.exp(jnp.log(10.0) * (jax.random.uniform(subkeys[1], (width_all, 1), jnp.float32) - 0.5))
    values_base = jax.random.truncated_normal(subkeys[2], -4.0, 4.0, (width_all, row_count), jnp.float32)
    return (values_base * row_scale[None, :] * col_scale * rising[None, :]).astype(jnp.float32)


def with_ends(drawn, stream_key, smallest, high):
    spot = [jax.random.randint(jax.random.fold_in(stream_key, axis), (), 0, length) for axis, length in enumerate(drawn.shape)]
    main_axis = drawn.shape.index(max(drawn.shape))
    neighbour = spot[:main_axis] + [(spot[main_axis] + 1) % drawn.shape[main_axis]] + spot[main_axis + 1:]
    return drawn.at[tuple(spot)].set(smallest).at[tuple(neighbour)].set(high)


def levels(rng, extent, cuts, least, high):
    def one(dim, parts):
        heights = jax.random.uniform(jax.random.fold_in(jax.random.fold_in(rng, 6), dim), (parts,), jnp.float32, least / len(cuts), high / len(cuts))
        return jnp.repeat(jnp.exp(heights), extent[dim] // parts).reshape((-1,) + (1,) * (len(extent) - dim - 1))

    level = one(*cuts[0])
    for cut in cuts[1:]:
        level = level * one(*cut)
    return level


def normal_values(key, shape, spread, most, cuts=(), kind=jnp.bfloat16):
    entries = jax.random.normal(key, shape, jnp.float32) * spread
    if len(cuts) > 0:
        entries = levels(key, shape, cuts, -0.22, 0.18) * entries
    return jnp.clip(entries, min=-most, max=most).astype(kind)


def setup_inputs(seed: int = 0) -> dict:
    key_list = jax.random.split(jax.random.key(seed), 5)
    return {
        "panels_in": draw_panels_in(jax.random.fold_in(key_list[4], 71), 0),
        "blocks": normal_values(key_list[1], (STEPS, NBLK, 3, BLOCK * BLOCK), (3 * BLOCK) ** -0.5, 0.4375, ((0, 8), (1, 32)), jnp.float32),
        "block_mask": with_ends((jax.random.randint(key_list[2], (STEPS, NBLK, 3), 0, 4) < 3).astype(jnp.int32), jax.random.fold_in(key_list[2], 1), 0, 1),
        "mixing": normal_values(key_list[3], (STEPS, PANELS, COLS, COLS), 0.15, 0.6, ((0, 8),), jnp.float32),
    }


def push_step(blocks_here, mask_here, current):
    count_blocks = current.shape[1] // BLOCK
    reshaped_block = current.reshape(current.shape[0], count_blocks, BLOCK)
    padded = jnp.pad(reshaped_block, ((0, 0), (1, 1), (0, 0)))
    mask_float = mask_here.astype(jnp.float32)
    pieces = jnp.stack([padded[:, offset:offset + count_blocks] for offset in range(3)], axis=2)
    pieces = pieces * mask_float[None, :, :, None]
    matrices = blocks_here.reshape(count_blocks, 3, BLOCK, BLOCK)
    result = jnp.einsum('bjik,cbjk->cbi', matrices, pieces, precision=lax.Precision.HIGHEST)
    return result.reshape(current.shape[0], count_blocks * BLOCK)

def pull_step(blocks_here, mask_here, current):
    count_blocks = current.shape[1] // BLOCK
    reshaped_block = current.reshape(current.shape[0], count_blocks, BLOCK)
    matrices = blocks_here.reshape(count_blocks, 3, BLOCK, BLOCK)
    products = jnp.einsum('bjik,cbi->cbjk', matrices, reshaped_block, precision=lax.Precision.HIGHEST)
    products = products * mask_here.astype(jnp.float32)[None, :, :, None]
    first_part = products[:, :, 0]
    middle_part = products[:, :, 1]
    last_part = products[:, :, 2]
    result = middle_part + jnp.pad(first_part[:, 1:], ((0, 0), (0, 1), (0, 0))) + jnp.pad(last_part[:, :-1], ((0, 0), (1, 0), (0, 0)))
    return result.reshape(current.shape[0], count_blocks * BLOCK)

def mix_columns(working, expansion_weights):
    panel_count = expansion_weights.shape[0]
    reshaped_block = working.reshape(panel_count, COLS, working.shape[1])
    blended_panel = jnp.einsum('yit,yif->ytf', expansion_weights, reshaped_block, precision=lax.Precision.HIGHEST)
    return working - blended_panel.reshape(working.shape)

def rescale(current):
    squares = lax.optimization_barrier(jnp.mean(current * current, axis=1, keepdims=True))
    return current / jnp.sqrt(squares + 1e-06)

def reference(panels_in, blocks, block_mask, mixing):
    current = panels_in
    forward_list = []
    for pair_index in range(N_TM):
        for offset in range(TRANSFER_RUN):
            step_index = pair_index * TRANSFER_RUN + offset
            current = mix_columns(push_step(blocks[step_index], block_mask[step_index], current), mixing[step_index])
        current = rescale(current)
        forward_list.append(current)
    adjoint_list = [None] * N_TM
    for pair_index in range(N_TM - 1, -1, -1):
        for offset in range(TRANSFER_RUN - 1, -1, -1):
            step_index = pair_index * TRANSFER_RUN + offset
            current = mix_columns(pull_step(blocks[step_index], block_mask[step_index], current), mixing[step_index])
        current = rescale(current)
        adjoint_list[pair_index] = current
    return (jnp.stack(forward_list), jnp.stack(adjoint_list))
```

```python
import functools

import jax
import jax.numpy as jnp
from jax import lax
from jax.experimental import pallas as pl
from jax.experimental.pallas import tpu as pltpu
from jax.sharding import PartitionSpec as P

BLOCK = 64
COLS = 8
PANELS = 4
ROWS = PANELS * COLS
TILE_BLOCKS = 8
TILE = TILE_BLOCKS * BLOCK
EDGE = 2 * BLOCK
LAG = 3
MESH = pl.DeviceIdType.MESH
F32 = jnp.float32
BF16 = jnp.bfloat16
HIGHEST = lax.Precision.HIGHEST


def halves(value):
    high = value.astype(BF16)
    low = (value - high.astype(F32)).astype(BF16)
    return high, low


def dot(a, b):
    return jnp.dot(a, b, preferred_element_type=F32)


def dot_exact(a, b):
    return jnp.dot(a, b, precision=HIGHEST, preferred_element_type=F32)


def dot_exact_nt(a, b):
    return lax.dot_general(
        a, b, (((1,), (1,)), ((), ())), precision=HIGHEST, preferred_element_type=F32
    )


def product(value, high, low):
    rows = value.shape[0]
    value_high, value_low = halves(value)
    both = dot(jnp.concatenate([value_high, value_low], axis=0), high)
    return both[:rows] + both[rows:] + dot(value_high, low)


def kernel(
    n_tm,
    n_space,
    near,
    panels_hbm,
    blocks_hbm,
    mask_ref,
    mixing_ref,
    forward_hbm,
    adjoint_hbm,
    raw,
    first,
    second,
    edge_low,
    edge_high,
    halo_low,
    halo_high,
    step_high,
    step_low,
    turned_high,
    turned_low,
    mix_forward,
    mix_adjoint,
    wide,
    state,
    spread,
    back,
    back_low,
    back_high,
    own_low,
    own_high,
    adjoint_state,
    gram_near,
    gram_far,
    chain_in,
    chain_out,
    scale_in,
    scale_out,
    result,
    local_sem,
    halo_send,
    halo_recv,
    wide_send,
    wide_recv,
    back_send,
    back_recv,
    own_send,
    own_recv,
    near_send,
    near_recv,
    far_send,
    far_recv,
    chain_send,
    chain_recv,
    scale_send,
    scale_recv,
):
    a = lax.axis_index("tm")
    s = lax.axis_index("space")
    far = n_space // near
    top = n_tm - 1
    near_base = (s // near) * near
    near_own = s % near
    far_own = s // near
    box_total = n_space * TILE
    has_left = s > 0
    has_right = s < n_space - 1

    barrier = pltpu.get_barrier_semaphore()

    def greet(condition, row, tile):
        @pl.when(condition)
        def _():
            pl.semaphore_signal(barrier, inc=1, device_id=(row, tile), device_id_type=MESH)

        return jnp.where(condition, 1, 0)

    greeted = jnp.int32(near - 1 + far - 1)
    for offset in range(1, near):
        tile = near_base + lax.rem(near_own + offset, near)
        pl.semaphore_signal(barrier, inc=1, device_id=(a, tile), device_id_type=MESH)
    for offset in range(1, far):
        tile = near_own + near * lax.rem(far_own + offset, far)
        pl.semaphore_signal(barrier, inc=1, device_id=(a, tile), device_id_type=MESH)
    for row_step in (-1, 0, 1):
        for tile_step in (-1, 0, 1):
            if row_step == 0 and tile_step == 0:
                continue
            row, tile = a + row_step, s + tile_step
            inside = (row >= 0) & (row <= top) & (tile >= 0) & (tile < n_space)
            greeted = greeted + greet(inside, row, tile)
    for condition, row in (
        (a <= top - LAG, a + LAG),
        (a >= LAG, a - LAG),
        (a == top - 2, a + 2),
        (a == top, a - 2),
    ):
        greeted = greeted + greet(condition, row, s)

    copy_blocks = pltpu.make_async_copy(blocks_hbm, raw, local_sem.at[0])
    copy_blocks.start()
    copy_panels = pltpu.make_async_copy(
        panels_hbm, wide.at[:, pl.ds(EDGE, TILE)], local_sem.at[1]
    )

    @pl.when(a == 0)
    def _():
        copy_panels.start()

    first[...] = jnp.zeros_like(first)
    second[...] = jnp.zeros_like(second)

    @pl.when(s == 0)
    def _():
        wide[:, 0:EDGE] = jnp.zeros((ROWS, EDGE), F32)
        halo_low[...] = jnp.zeros_like(halo_low)

    @pl.when(s == n_space - 1)
    def _():
        wide[:, EDGE + TILE : 2 * EDGE + TILE] = jnp.zeros((ROWS, EDGE), F32)
        halo_high[...] = jnp.zeros_like(halo_high)

    lane = lax.broadcasted_iota(jnp.int32, (32, 128), 1)
    is_left = lane < BLOCK

    def pair(left, right):
        if left is None:
            even = jnp.where(is_left, 0.0, pltpu.roll(right, BLOCK, 1))
            odd = jnp.where(is_left, 0.0, right)
        elif right is None:
            even = jnp.where(is_left, left, 0.0)
            odd = jnp.where(is_left, pltpu.roll(left, BLOCK, 1), 0.0)
        else:
            even = jnp.where(is_left, left, pltpu.roll(right, BLOCK, 1))
            odd = jnp.where(is_left, pltpu.roll(left, BLOCK, 1), right)
        return even, odd

    def put(target, row, values):
        for parity in range(2):
            target[pl.ds(row + parity, 32, stride=2), :] = values[parity]

    def lanes(ref, start, stop, row, rows):
        tiles = [ref[tile, row : row + rows, :] for tile in range(start, stop)]
        return jnp.concatenate(tiles, axis=1)

    copy_blocks.wait()
    for step in range(2):
        for block in range(TILE_BLOCKS):
            packed = []
            for j in range(3):
                start = (step * 3 + j) * 256 + block
                scale = mask_ref[step * 24 + block * 3 + j].astype(F32)
                packed.append(raw[pl.ds(start, 32, stride=8), :] * scale)
            if block % 2 == 0:
                tiles = [(None, packed[0]), (packed[1], packed[2])]
                tile_index = block // 2 - 1
            else:
                tiles = [(packed[0], packed[1]), (packed[2], None)]
                tile_index = (block - 1) // 2
            for extra in range(2):
                values = pair(*tiles[extra])
                index = tile_index + extra
                if step == 0:
                    put(first.at[index + 1], block * BLOCK, values)
                elif index < 0:
                    put(edge_low, 0, values)
                elif index >= TILE // 128:
                    put(edge_high, 0, values)
                else:
                    put(second.at[index], block * BLOCK, values)

    pl.semaphore_wait(barrier, greeted)

    send_right = pltpu.make_async_remote_copy(
        src_ref=first.at[pl.ds(4, 2), pl.ds(TILE - BLOCK, BLOCK)],
        dst_ref=halo_low,
        send_sem=halo_send.at[0],
        recv_sem=halo_recv.at[0],
        device_id=(a, s + 1),
        device_id_type=MESH,
    )
    send_left = pltpu.make_async_remote_copy(
        src_ref=first.at[pl.ds(0, 2), pl.ds(0, BLOCK)],
        dst_ref=halo_high,
        send_sem=halo_send.at[1],
        recv_sem=halo_recv.at[1],
        device_id=(a, s - 1),
        device_id_type=MESH,
    )

    def copies_wide(source, row, base):
        center = pltpu.make_async_remote_copy(
            src_ref=source,
            dst_ref=wide.at[:, pl.ds(EDGE, TILE)],
            send_sem=wide_send.at[base],
            recv_sem=wide_recv.at[0],
            device_id=(row, s),
            device_id_type=MESH,
        )
        right = pltpu.make_async_remote_copy(
            src_ref=source.at[:, pl.ds(TILE - EDGE, EDGE)],
            dst_ref=wide.at[:, pl.ds(0, EDGE)],
            send_sem=wide_send.at[base + 1],
            recv_sem=wide_recv.at[1],
            device_id=(row, s + 1),
            device_id_type=MESH,
        )
        left = pltpu.make_async_remote_copy(
            src_ref=source.at[:, pl.ds(0, EDGE)],
            dst_ref=wide.at[:, pl.ds(EDGE + TILE, EDGE)],
            send_sem=wide_send.at[base + 2],
            recv_sem=wide_recv.at[2],
            device_id=(row, s - 1),
            device_id_type=MESH,
        )
        return center, right, left

    _, panel_right, panel_left = copies_wide(panels_hbm, a, 0)
    state_center, state_right, state_left = copies_wide(state, a + 1, 3)

    @pl.when((a == 0) & has_right)
    def _():
        panel_right.start()

    @pl.when((a == 0) & has_left)
    def _():
        panel_left.start()

    @pl.when(has_right)
    def _():
        send_right.start()

    @pl.when(has_left)
    def _():
        send_left.start()

    def formed(group):
        mid = 128 * group
        left = lanes(second, group, group + 3, 256 * group, 256)
        right = lanes(first, 2 * group, 2 * group + 4, mid, 384)
        right_high, right_low = halves(right)
        return product(left, right_high, right_low)

    group_low = formed(0)
    group_high = formed(1)

    row_index = lax.broadcasted_iota(jnp.int32, (ROWS, ROWS), 0)
    col_index = lax.broadcasted_iota(jnp.int32, (ROWS, ROWS), 1)
    same_panel = row_index // COLS == col_index // COLS
    eye = jnp.where(row_index == col_index, 1.0, 0.0).astype(F32)
    spread_rows = lax.broadcasted_iota(jnp.int32, (COLS, ROWS), 0)
    spread_cols = lax.broadcasted_iota(jnp.int32, (COLS, ROWS), 1)
    repeat = jnp.where(spread_cols % COLS == spread_rows, 1.0, 0.0).astype(F32)

    def mixer(step):
        stacked = jnp.concatenate([mixing_ref[step, p] for p in range(PANELS)], axis=0)
        return eye - jnp.where(same_panel, dot_exact(stacked, repeat), 0.0)

    mixer_first = mixer(0)
    mixer_second = mixer(1)
    mix_forward[...] = dot_exact_nt(eye, dot_exact(mixer_first, mixer_second))
    mix_adjoint[...] = dot_exact_nt(eye, dot_exact(mixer_second, mixer_first))

    @pl.when(has_left)
    def _():
        send_right.wait_recv()

    @pl.when(has_right)
    def _():
        send_left.wait_recv()

    beside_high, beside_low = halves(lanes(halo_low, 0, 2, 0, BLOCK))
    add_low = product(pltpu.roll(edge_low[...], BLOCK, 1)[:, :BLOCK], beside_high, beside_low)
    beside_high, beside_low = halves(lanes(halo_high, 0, 2, 0, BLOCK))
    add_high = product(edge_high[...][:, :BLOCK], beside_high, beside_low)
    group_low = jnp.concatenate(
        [
            jnp.concatenate([group_low[:BLOCK, :256] + add_low, group_low[:BLOCK, 256:]], axis=1),
            group_low[BLOCK:],
        ],
        axis=0,
    )
    group_high = jnp.concatenate(
        [
            group_high[: 256 - BLOCK],
            jnp.concatenate(
                [group_high[256 - BLOCK :, :256], group_high[256 - BLOCK :, 256:] + add_high],
                axis=1,
            ),
        ],
        axis=0,
    )
    for group, value in enumerate((group_low, group_high)):
        turned = jnp.transpose(value)
        turned_high[group], turned_low[group] = halves(turned)
        step_high[group], step_low[group] = halves(value)

    adjoint_center = pltpu.make_async_remote_copy(
        src_ref=spread.at[:, pl.ds(EDGE, TILE)],
        dst_ref=back,
        send_sem=back_send.at[0],
        recv_sem=back_recv.at[0],
        device_id=(a - 1, s),
        device_id_type=MESH,
    )

    def copies_edge(row, into_low, into_high, send_sems, recv_sems, base):
        right = pltpu.make_async_remote_copy(
            src_ref=spread.at[:, pl.ds(EDGE + TILE, EDGE)],
            dst_ref=into_low,
            send_sem=send_sems.at[base],
            recv_sem=recv_sems.at[base],
            device_id=(row, s + 1),
            device_id_type=MESH,
        )
        left = pltpu.make_async_remote_copy(
            src_ref=spread.at[:, pl.ds(0, EDGE)],
            dst_ref=into_high,
            send_sem=send_sems.at[base + 1],
            recv_sem=recv_sems.at[base + 1],
            device_id=(row, s - 1),
            device_id_type=MESH,
        )
        return right, left

    adjoint_right, adjoint_left = copies_edge(a - 1, back_low, back_high, back_send, back_recv, 1)
    own_right, own_left = copies_edge(a, own_low, own_high, own_send, own_recv, 0)

    def near_copy(pass_index, offset):
        tile = near_base + lax.rem(near_own + offset, near)
        return pltpu.make_async_remote_copy(
            src_ref=gram_near.at[pass_index, near_own],
            dst_ref=gram_near.at[pass_index, near_own],
            send_sem=near_send.at[pass_index, offset],
            recv_sem=near_recv.at[pass_index, near - offset],
            device_id=(a, tile),
            device_id_type=MESH,
        )

    def far_copy(pass_index, offset):
        tile = near_own + near * lax.rem(far_own + offset, far)
        return pltpu.make_async_remote_copy(
            src_ref=gram_far.at[pass_index, far_own],
            dst_ref=gram_far.at[pass_index, far_own],
            send_sem=far_send.at[pass_index, offset],
            recv_sem=far_recv.at[pass_index, far - offset],
            device_id=(a, tile),
            device_id_type=MESH,
        )

    def chain_copy(pass_index, target_pass, row):
        return pltpu.make_async_remote_copy(
            src_ref=chain_out.at[pass_index],
            dst_ref=chain_in.at[target_pass],
            send_sem=chain_send.at[pass_index],
            recv_sem=chain_recv.at[target_pass],
            device_id=(row, s),
            device_id_type=MESH,
        )

    def scale_copy(pass_index, target_pass, row):
        return pltpu.make_async_remote_copy(
            src_ref=scale_out.at[pass_index],
            dst_ref=scale_in.at[target_pass],
            send_sem=scale_send.at[pass_index],
            recv_sem=scale_recv.at[target_pass],
            device_id=(row, s),
            device_id_type=MESH,
        )

    def send_gram(pass_index, value):
        gram = dot_exact_nt(value, value)
        wide_gram = jnp.concatenate([gram, jnp.zeros((ROWS, 128 - ROWS), F32)], axis=1)
        rows_wide = lax.broadcasted_iota(jnp.int32, (ROWS, 128), 0)
        cols_wide = lax.broadcasted_iota(jnp.int32, (ROWS, 128), 1)
        kept = jnp.where(rows_wide // COLS == cols_wide // COLS, wide_gram, 0.0)
        compact = kept[0:COLS]
        for p in range(1, PANELS):
            compact = compact + kept[p * COLS : (p + 1) * COLS]
        gram_near[pass_index, near_own] = compact
        for offset in range(1, near):
            near_copy(pass_index, offset).start()

    def reduce_gram(pass_index):
        for offset in range(1, near):
            near_copy(pass_index, near - offset).wait_recv()
        total = gram_near[pass_index, 0]
        for slot in range(1, near):
            total = total + gram_near[pass_index, slot]
        gram_far[pass_index, far_own] = total
        for offset in range(1, far):
            far_copy(pass_index, offset).start()
        for offset in range(1, far):
            far_copy(pass_index, far - offset).wait_recv()
        total = gram_far[pass_index, 0]
        for slot in range(1, far):
            total = total + gram_far[pass_index, slot]
        return total

    def finish(pass_index, gram_sum, mix_ref, value_ref, out_copy):
        rows_wide = lax.broadcasted_iota(jnp.int32, (ROWS, 128), 0)
        cols_wide = lax.broadcasted_iota(jnp.int32, (ROWS, 128), 1)
        gram = jnp.where(
            rows_wide // COLS == cols_wide // COLS,
            jnp.concatenate([gram_sum] * PANELS, axis=0) / box_total,
            0.0,
        )
        size = jnp.sum(jnp.where(rows_wide == cols_wide, gram, 0.0)) / ROWS
        size = jnp.sqrt(jnp.full((8, 128), size, F32))
        before = chain_in[pass_index, 0:ROWS]
        size_before = chain_in[pass_index, ROWS : ROWS + 8]
        scale = scale_in[pass_index]
        mixed = dot_exact(mix_ref[...], before) / scale[0:1, :]
        squares = jnp.sum(dot_exact(mixed[:, :ROWS], gram) * mixed, axis=1, keepdims=True)
        combined = mixed / jnp.sqrt(jnp.maximum(squares, 0.0) + 1e-06)
        chain_out[pass_index, 0:ROWS] = combined
        chain_out[pass_index, ROWS : ROWS + 8] = size
        usable = (size > 1e-30) & (size_before > 1e-30)
        ratio = scale * (size_before / jnp.where(usable, size, 1.0))
        scale_out[pass_index] = jnp.where(usable, jnp.clip(ratio, 1e-12, 1e12), 1.0)
        return combined

    def emit(pass_index, combined, value_ref):
        result[pass_index] = dot_exact(combined[:, :ROWS], value_ref[...])

    out_forward = pltpu.make_async_copy(result.at[0], forward_hbm.at[0], local_sem.at[2])
    out_adjoint = pltpu.make_async_copy(result.at[1], adjoint_hbm.at[0], local_sem.at[3])

    lanes_eye = lax.broadcasted_iota(jnp.int32, (ROWS + 8, 128), 1)
    rows_eye = lax.broadcasted_iota(jnp.int32, (ROWS + 8, 128), 0)

    @pl.when(a == 0)
    def _():
        chain_in[0] = jnp.where((rows_eye == lanes_eye) | (rows_eye >= ROWS), 1.0, 0.0)
        copy_panels.wait()

    @pl.when(a < LAG)
    def _():
        scale_in[0] = jnp.ones((8, 128), F32)

    @pl.when(a >= LAG)
    def _():
        scale_copy(0, 0, a).wait_recv()

    @pl.when(a > 0)
    def _():
        state_center.wait_recv()

    @pl.when(has_left)
    def _():
        state_right.wait_recv()

    @pl.when(has_right)
    def _():
        state_left.wait_recv()

    for group in range(2):
        value = wide[:, 256 * group : 256 * group + 512]
        moved = product(value, turned_high[group], turned_low[group])
        state[:, 256 * group : 256 * group + 256] = moved * scale_in[0, 0:1, 0:1]

    @pl.when(a < top)
    def _():
        state_center.start()

    @pl.when((a < top) & has_right)
    def _():
        state_right.start()

    @pl.when((a < top) & has_left)
    def _():
        state_left.start()

    send_gram(0, state[...])

    def adjoint_apply(value):
        parts = []
        for group in range(2):
            parts.append(
                product(
                    value[:, 256 * group : 256 * group + 256], step_high[group], step_low[group]
                )
            )
        scale = scale_in[1, 0:1, 0:1]
        spread[:, 0:256] = parts[0][:, 0:256] * scale
        spread[:, 256:512] = (parts[0][:, 256:512] + parts[1][:, 0:256]) * scale
        spread[:, 512:768] = parts[1][:, 256:512] * scale

        @pl.when(a > 0)
        def _():
            adjoint_center.start()

        @pl.when((a > 0) & has_right)
        def _():
            adjoint_right.start()

        @pl.when((a > 0) & has_left)
        def _():
            adjoint_left.start()

        @pl.when(has_right)
        def _():
            own_right.start()

        @pl.when(has_left)
        def _():
            own_left.start()

        @pl.when(has_left)
        def _():
            own_right.wait_recv()

        @pl.when(has_right)
        def _():
            own_left.wait_recv()

        adjoint_state[...] = spread[:, EDGE : EDGE + TILE]

        @pl.when(has_left)
        def _():
            adjoint_state[:, 0:EDGE] = adjoint_state[:, 0:EDGE] + own_low[...]

        @pl.when(has_right)
        def _():
            adjoint_state[:, TILE - EDGE : TILE] = (
                adjoint_state[:, TILE - EDGE : TILE] + own_high[...]
            )

        send_gram(1, adjoint_state[...])

    @pl.when(a == top)
    def _():
        scale_copy(0, 1, a).wait_recv()
        adjoint_apply(state[...])

    forward_sum = reduce_gram(0)

    @pl.when(a > 0)
    def _():
        chain_copy(0, 0, a).wait_recv()

    forward_combined = finish(0, forward_sum, mix_forward, state, None)

    @pl.when(a < top)
    def _():
        chain_copy(0, 0, a + 1).start()

    @pl.when(a <= top - LAG)
    def _():
        scale_copy(0, 0, a + LAG).start()

    @pl.when(a == top - 2)
    def _():
        scale_copy(0, 1, a + 2).start()

    @pl.when(a == top)
    def _():
        scale_copy(0, 1, a - 2).start()
        chain_in[1] = chain_out[0]

    @pl.when(a == top - 1)
    def _():
        scale_in[1] = scale_out[0]

    emit(0, forward_combined, state)
    out_forward.start()

    @pl.when(a < top)
    def _():
        @pl.when(a != top - 1)
        def _():
            scale_copy(0, 1, a).wait_recv()

        adjoint_center.wait_recv()

        @pl.when(has_left)
        def _():
            adjoint_right.wait_recv()
            back[:, 0:EDGE] = back[:, 0:EDGE] + back_low[...]

        @pl.when(has_right)
        def _():
            adjoint_left.wait_recv()
            back[:, TILE - EDGE : TILE] = back[:, TILE - EDGE : TILE] + back_high[...]

        adjoint_apply(back[...])

    adjoint_sum = reduce_gram(1)

    @pl.when(a < top)
    def _():
        chain_copy(1, 1, a).wait_recv()

    adjoint_combined = finish(1, adjoint_sum, mix_adjoint, adjoint_state, None)

    @pl.when(a > 0)
    def _():
        chain_copy(1, 1, a - 1).start()

    @pl.when(a >= LAG)
    def _():
        scale_copy(1, 1, a - LAG).start()

    emit(1, adjoint_combined, adjoint_state)
    out_adjoint.start()

    @pl.when(has_right)
    def _():
        send_right.wait_send()
        own_right.wait_send()

    @pl.when(has_left)
    def _():
        send_left.wait_send()
        own_left.wait_send()

    @pl.when((a == 0) & has_right)
    def _():
        panel_right.wait_send()

    @pl.when((a == 0) & has_left)
    def _():
        panel_left.wait_send()

    @pl.when(a < top)
    def _():
        state_center.wait_send()
        chain_copy(0, 0, a + 1).wait_send()

    @pl.when((a < top) & has_right)
    def _():
        state_right.wait_send()

    @pl.when((a < top) & has_left)
    def _():
        state_left.wait_send()

    @pl.when(a > 0)
    def _():
        adjoint_center.wait_send()
        chain_copy(1, 1, a - 1).wait_send()

    @pl.when((a > 0) & has_right)
    def _():
        adjoint_right.wait_send()

    @pl.when((a > 0) & has_left)
    def _():
        adjoint_left.wait_send()

    @pl.when(a != top - 1)
    def _():
        scale_copy(0, 0, a).wait_send()

    @pl.when(a >= LAG)
    def _():
        scale_copy(1, 1, a).wait_send()

    for pass_index in range(2):
        for offset in range(1, near):
            near_copy(pass_index, offset).wait_send()
        for offset in range(1, far):
            far_copy(pass_index, offset).wait_send()
    out_forward.wait()
    out_adjoint.wait()


def solution(mesh):
    n_tm = mesh.shape["tm"]
    n_space = mesh.shape["space"]
    near = min(8, n_space) if n_space >= 8 else 2
    far = n_space // near

    def shards(panels_in, blocks, block_mask, mixing):
        lines = blocks.reshape(2, TILE_BLOCKS, 3, 32, 128).transpose(0, 2, 3, 1, 4)
        lines = lines.reshape(2 * 3 * 32 * TILE_BLOCKS, 128)
        dma = pltpu.SemaphoreType.DMA
        vmem = pltpu.VMEM
        scratch = [
            vmem((2 * 3 * 32 * TILE_BLOCKS, 128), F32),
            vmem((6, TILE, 128), F32),
            vmem((4, TILE, 128), F32),
            vmem((BLOCK, 128), F32),
            vmem((BLOCK, 128), F32),
            vmem((2, BLOCK, 128), F32),
            vmem((2, BLOCK, 128), F32),
            vmem((2, 256, 512), BF16),
            vmem((2, 256, 512), BF16),
            vmem((2, 512, 256), BF16),
            vmem((2, 512, 256), BF16),
            vmem((ROWS, ROWS), F32),
            vmem((ROWS, ROWS), F32),
            vmem((ROWS, TILE + 2 * EDGE), F32),
            vmem((ROWS, TILE), F32),
            vmem((ROWS, TILE + 2 * EDGE), F32),
            vmem((ROWS, TILE), F32),
            vmem((ROWS, EDGE), F32),
            vmem((ROWS, EDGE), F32),
            vmem((ROWS, EDGE), F32),
            vmem((ROWS, EDGE), F32),
            vmem((ROWS, TILE), F32),
            vmem((2, near, 8, 128), F32),
            vmem((2, far, 8, 128), F32),
            vmem((2, ROWS + 8, 128), F32),
            vmem((2, ROWS + 8, 128), F32),
            vmem((2, 8, 128), F32),
            vmem((2, 8, 128), F32),
            vmem((2, ROWS, TILE), F32),
            dma((4,)),
            dma((2,)),
            dma((2,)),
            dma((6,)),
            dma((3,)),
            dma((3,)),
            dma((3,)),
            dma((2,)),
            dma((2,)),
            dma((2, near)),
            dma((2, near)),
            dma((2, far)),
            dma((2, far)),
            dma((2,)),
            dma((2,)),
            dma((2,)),
            dma((2,)),
        ]
        shape = jax.ShapeDtypeStruct((1, ROWS, TILE), F32)
        return pl.pallas_call(
            functools.partial(kernel, n_tm, n_space, near),
            out_shape=(shape, shape),
            in_specs=[
                pl.BlockSpec(memory_space=pl.ANY),
                pl.BlockSpec(memory_space=pl.ANY),
                pl.BlockSpec(memory_space=pltpu.SMEM),
                pl.BlockSpec(memory_space=pltpu.VMEM),
            ],
            out_specs=(pl.BlockSpec(memory_space=pl.ANY), pl.BlockSpec(memory_space=pl.ANY)),
            scratch_shapes=scratch,
            compiler_params=pltpu.CompilerParams(collective_id=0, has_side_effects=True),
        )(panels_in, lines, block_mask.reshape(-1), mixing)

    return jax.shard_map(
        shards,
        mesh=mesh,
        in_specs=(
            P(None, "space"),
            P("tm", "space", None, None),
            P("tm", "space", None),
            P("tm", None, None, None),
        ),
        out_specs=(P("tm", None, "space"), P("tm", None, "space")),
        check_vma=False,
    )
```

```python
import functools

import jax
import jax.numpy as jnp
from jax import lax
from jax.experimental import pallas as pl
from jax.experimental.pallas import tpu as pltpu
from jax.sharding import PartitionSpec as P

BLOCK = 64
COLS = 8
PANELS = 4
ROWS = PANELS * COLS
TILE_BLOCKS = 8
TILE = TILE_BLOCKS * BLOCK
EDGE = 2 * BLOCK
LAG = 4
STRIP = EDGE + 2 * EDGE
START = 2.0**-10
MESH = pl.DeviceIdType.MESH
F32 = jnp.float32
BF16 = jnp.bfloat16
HIGHEST = lax.Precision.HIGHEST


def halves(value):
    high = value.astype(BF16)
    low = (value - high.astype(F32)).astype(BF16)
    return high, low


def dot(a, b):
    return jnp.dot(a, b, preferred_element_type=F32)


def dot_exact(a, b):
    return jnp.dot(a, b, precision=HIGHEST, preferred_element_type=F32)


def dot_exact_nt(a, b):
    return lax.dot_general(
        a, b, (((1,), (1,)), ((), ())), precision=HIGHEST, preferred_element_type=F32
    )


def product(value, high, low):
    rows = value.shape[0]
    value_high, value_low = halves(value)
    both = dot(jnp.concatenate([value_high, value_low], axis=0), high)
    return both[:rows] + both[rows:] + dot(value_high, low)


def kernel(
    n_tm,
    n_space,
    near,
    panels_hbm,
    blocks_hbm,
    mask_ref,
    mixing_ref,
    forward_hbm,
    adjoint_hbm,
    raw,
    first,
    second,
    edge_low,
    edge_high,
    halo_low,
    halo_high,
    band,
    beside,
    turned,
    operator_high,
    operator_low,
    strip_in,
    wide,
    source_low,
    source_high,
    state,
    gram_near,
    gram_far,
    sums,
    combined_ref,
    size_ref,
    scale_ref,
    result,
    local_sem,
    halo_send,
    halo_recv,
    beside_send,
    beside_recv,
    strip_send,
    strip_recv,
    wide_send,
    wide_recv,
    source_send,
    source_recv,
    near_send,
    near_recv,
    far_send,
    far_recv,
    sums_send,
    sums_recv,
):
    a = lax.axis_index("tm")
    s = lax.axis_index("space")
    far = n_space // near
    top = n_tm - 1
    last = 2 * n_tm - 1 - a
    near_base = (s // near) * near
    near_own = s % near
    far_own = s // near
    box_total = n_space * TILE
    has_left = s > 0
    has_right = s < n_space - 1
    always = a >= 0

    barrier = pltpu.get_barrier_semaphore()

    def greet(condition, row, tile):
        @pl.when(condition)
        def _():
            pl.semaphore_signal(barrier, inc=1, device_id=(row, tile), device_id_type=MESH)

        return jnp.where(condition, 1, 0)

    greeted = jnp.int32(near - 1 + far - 1 + n_tm - 1)
    for offset in range(1, near):
        tile = near_base + lax.rem(near_own + offset, near)
        pl.semaphore_signal(barrier, inc=1, device_id=(a, tile), device_id_type=MESH)
    for offset in range(1, far):
        tile = near_own + near * lax.rem(far_own + offset, far)
        pl.semaphore_signal(barrier, inc=1, device_id=(a, tile), device_id_type=MESH)
    for offset in range(1, n_tm):
        row = lax.rem(a + offset, n_tm)
        pl.semaphore_signal(barrier, inc=1, device_id=(row, s), device_id_type=MESH)
    for row_step in (-2, -1, 0, 1, 2):
        for tile_step in (-1, 1):
            row, tile = a + row_step, s + tile_step
            inside = (row >= 0) & (row <= top) & (tile >= 0) & (tile < n_space)
            greeted = greeted + greet(inside, row, tile)

    copy_blocks = pltpu.make_async_copy(blocks_hbm, raw, local_sem.at[0])
    copy_blocks.start()
    copy_panels = pltpu.make_async_copy(
        panels_hbm, wide.at[0, :, pl.ds(EDGE, TILE)], local_sem.at[1]
    )

    @pl.when(a == 0)
    def _():
        copy_panels.start()

    sent = []

    def send(condition, copy):
        sent.append((condition, copy))

        @pl.when(condition)
        def _():
            copy.start()

    def receive(condition, copy):
        @pl.when(condition)
        def _():
            copy.wait_recv()

    def remote(source, target, send_sem, recv_sem, row, tile):
        return pltpu.make_async_remote_copy(
            src_ref=source,
            dst_ref=target,
            send_sem=send_sem,
            recv_sem=recv_sem,
            device_id=(row, tile),
            device_id_type=MESH,
        )

    first[...] = jnp.zeros_like(first)
    second[...] = jnp.zeros_like(second)
    scale_ref[...] = jnp.ones_like(scale_ref)
    scale_ref[0] = jnp.full((8, 128), START, F32)
    size_ref[...] = jnp.full((8, 128), 1.0 / START, F32)
    rows_eye = lax.broadcasted_iota(jnp.int32, (ROWS, 128), 0)
    cols_eye = lax.broadcasted_iota(jnp.int32, (ROWS, 128), 1)
    combined_ref[...] = jnp.where(rows_eye == cols_eye, 1.0, 0.0)

    @pl.when(s == 0)
    def _():
        for pass_index in range(2):
            wide[pass_index, :, 0:EDGE] = jnp.zeros((ROWS, EDGE), F32)
        halo_low[...] = jnp.zeros_like(halo_low)
        beside[0] = jnp.zeros((EDGE, EDGE), F32)

    @pl.when(s == n_space - 1)
    def _():
        for pass_index in range(2):
            wide[pass_index, :, EDGE + TILE : 2 * EDGE + TILE] = jnp.zeros((ROWS, EDGE), F32)
        halo_high[...] = jnp.zeros_like(halo_high)
        beside[1] = jnp.zeros((EDGE, EDGE), F32)

    lane = lax.broadcasted_iota(jnp.int32, (32, 128), 1)
    is_left = lane < BLOCK

    def pair(left, right):
        if left is None:
            even = jnp.where(is_left, 0.0, pltpu.roll(right, BLOCK, 1))
            odd = jnp.where(is_left, 0.0, right)
        elif right is None:
            even = jnp.where(is_left, left, 0.0)
            odd = jnp.where(is_left, pltpu.roll(left, BLOCK, 1), 0.0)
        else:
            even = jnp.where(is_left, left, pltpu.roll(right, BLOCK, 1))
            odd = jnp.where(is_left, pltpu.roll(left, BLOCK, 1), right)
        return even, odd

    def put(target, row, values):
        for parity in range(2):
            target[pl.ds(row + parity, 32, stride=2), :] = values[parity]

    def lanes(ref, start, stop, row, rows):
        tiles = [ref[tile, row : row + rows, :] for tile in range(start, stop)]
        return jnp.concatenate(tiles, axis=1)

    copy_blocks.wait()
    for step in range(2):
        for block in range(TILE_BLOCKS):
            packed = []
            for j in range(3):
                start = (step * 3 + j) * 256 + block
                scale = mask_ref[j, step, block].astype(F32)
                packed.append(raw[pl.ds(start, 32, stride=8), :] * scale)
            if block % 2 == 0:
                tiles = [(None, packed[0]), (packed[1], packed[2])]
                tile_index = block // 2 - 1
            else:
                tiles = [(packed[0], packed[1]), (packed[2], None)]
                tile_index = (block - 1) // 2
            for extra in range(2):
                values = pair(*tiles[extra])
                index = tile_index + extra
                if step == 0:
                    put(first.at[index + 1], block * BLOCK, values)
                elif index < 0:
                    put(edge_low, 0, values)
                elif index >= TILE // 128:
                    put(edge_high, 0, values)
                else:
                    put(second.at[index], block * BLOCK, values)

    pl.semaphore_wait(barrier, greeted)

    def copies_direct(source, row, base):
        right = remote(
            source.at[:, pl.ds(TILE - EDGE, EDGE)],
            wide.at[0, :, pl.ds(0, EDGE)],
            wide_send.at[base],
            wide_recv.at[2],
            row,
            s + 1,
        )
        left = remote(
            source.at[:, pl.ds(0, EDGE)],
            wide.at[0, :, pl.ds(EDGE + TILE, EDGE)],
            wide_send.at[base + 1],
            wide_recv.at[3],
            row,
            s - 1,
        )
        return right, left

    panel_right, panel_left = copies_direct(panels_hbm, a, 2)
    state_right, state_left = copies_direct(state.at[0], a + 1, 4)
    send(has_right & (a == 0), panel_right)
    send(has_left & (a == 0), panel_left)
    halo_right = remote(
        first.at[pl.ds(4, 2), pl.ds(TILE - BLOCK, BLOCK)],
        halo_low,
        halo_send.at[0],
        halo_recv.at[0],
        a,
        s + 1,
    )
    halo_left = remote(
        first.at[pl.ds(0, 2), pl.ds(0, BLOCK)],
        halo_high,
        halo_send.at[1],
        halo_recv.at[1],
        a,
        s - 1,
    )
    send(has_right, halo_right)
    send(has_left, halo_left)

    def formed(group):
        mid = 128 * group
        left = lanes(second, group, group + 3, 256 * group, 256)
        right = lanes(first, 2 * group, 2 * group + 4, mid, 384)
        right_high, right_low = halves(right)
        return product(left, right_high, right_low)

    group_low = formed(0)
    group_high = formed(1)

    row_index = lax.broadcasted_iota(jnp.int32, (ROWS, ROWS), 0)
    col_index = lax.broadcasted_iota(jnp.int32, (ROWS, ROWS), 1)
    same_panel = row_index // COLS == col_index // COLS
    eye = jnp.where(row_index == col_index, 1.0, 0.0).astype(F32)
    spread_rows = lax.broadcasted_iota(jnp.int32, (COLS, ROWS), 0)
    spread_cols = lax.broadcasted_iota(jnp.int32, (COLS, ROWS), 1)
    repeat = jnp.where(spread_cols % COLS == spread_rows, 1.0, 0.0).astype(F32)
    panel_wide = rows_eye // COLS == cols_eye // COLS

    def mixer(step):
        stacked = jnp.concatenate([mixing_ref[step, p] for p in range(PANELS)], axis=0)
        return eye - jnp.where(same_panel, dot_exact(stacked, repeat), 0.0)

    def compact(value):
        padded = jnp.concatenate([value, jnp.zeros((ROWS, 128 - ROWS), F32)], axis=1)
        kept = jnp.where(panel_wide, padded, 0.0)
        total = kept[0:COLS]
        for p in range(1, PANELS):
            total = total + kept[p * COLS : (p + 1) * COLS]
        return total

    def expand(value):
        return jnp.where(panel_wide, jnp.concatenate([value] * PANELS, axis=0), 0.0)

    mixer_first = mixer(0)
    mixer_second = mixer(1)
    sums[a, COLS : 2 * COLS] = compact(dot_exact_nt(eye, dot_exact(mixer_first, mixer_second)))
    sums[last, COLS : 2 * COLS] = compact(dot_exact_nt(eye, dot_exact(mixer_second, mixer_first)))

    receive(has_left, halo_right)
    receive(has_right, halo_left)

    beside_high, beside_low = halves(lanes(halo_low, 0, 2, 0, BLOCK))
    add_low = product(pltpu.roll(edge_low[...], BLOCK, 1)[:, :BLOCK], beside_high, beside_low)
    beside_high, beside_low = halves(lanes(halo_high, 0, 2, 0, BLOCK))
    add_high = product(edge_high[...][:, :BLOCK], beside_high, beside_low)
    band[0] = group_low
    band[1] = group_high
    band[0, 0:BLOCK, 0:256] = group_low[:BLOCK, :256] + add_low
    band[1, 256 - BLOCK : 256, 256:512] = group_high[256 - BLOCK :, 256:] + add_high

    for group in range(2):
        value = jnp.transpose(band[group])
        turned[0, group] = value
        operator_high[0, group], operator_low[0, group] = halves(value)

    beside_right = remote(
        band.at[1, pl.ds(EDGE, EDGE), pl.ds(384, EDGE)],
        beside.at[0],
        beside_send.at[0],
        beside_recv.at[0],
        a,
        s + 1,
    )
    beside_left = remote(
        band.at[0, pl.ds(0, EDGE), pl.ds(0, EDGE)],
        beside.at[1],
        beside_send.at[1],
        beside_recv.at[1],
        a,
        s - 1,
    )

    def copies_strip(source_pass, row, target_pass):
        right = remote(
            turned.at[source_pass, 1, pl.ds(EDGE, STRIP), pl.ds(EDGE, EDGE)],
            strip_in.at[target_pass, 0],
            strip_send.at[source_pass, 0],
            strip_recv.at[target_pass, 0],
            row,
            s + 1,
        )
        left = remote(
            turned.at[source_pass, 0, pl.ds(0, STRIP), pl.ds(0, EDGE)],
            strip_in.at[target_pass, 1],
            strip_send.at[source_pass, 1],
            strip_recv.at[target_pass, 1],
            row,
            s - 1,
        )
        return right, left

    def send_operator():
        strip_right, strip_left = copies_strip(
            0, jnp.minimum(a + 1, top), jnp.where(a < top, 0, 1)
        )
        send((a > 0) & has_right, strip_right)
        send((a > 0) & has_left, strip_left)
        send(has_right, beside_right)
        send(has_left, beside_left)

    strip_adjoint_right, strip_adjoint_left = copies_strip(1, a - 1, 1)

    def prepare_adjoint():
        receive(has_left, beside_right)
        receive(has_right, beside_left)
        blank = jnp.zeros((EDGE, EDGE), F32)
        turned[1, 0, 0:EDGE] = jnp.concatenate([beside[0], blank], axis=1)
        turned[1, 0, EDGE : EDGE + 256] = band[0, :, EDGE : EDGE + 256]
        turned[1, 0, 384:512] = jnp.concatenate([blank, band[1, 0:EDGE, 0:EDGE]], axis=1)
        turned[1, 1, 0:EDGE] = jnp.concatenate([band[0, EDGE : 2 * EDGE, 384:512], blank], axis=1)
        turned[1, 1, EDGE : EDGE + 256] = band[1, :, EDGE : EDGE + 256]
        turned[1, 1, 384:512] = jnp.concatenate([blank, beside[1]], axis=1)
        for group in range(2):
            operator_high[1, group], operator_low[1, group] = halves(turned[1, group])

        @pl.when((a > 0) & has_right)
        def _():
            strip_adjoint_right.start()

        @pl.when((a > 0) & has_left)
        def _():
            strip_adjoint_left.start()

    sent.append(((a > 0) & has_right, strip_adjoint_right))
    sent.append(((a > 0) & has_left, strip_adjoint_left))

    def near_copy(pass_index, offset):
        tile = near_base + lax.rem(near_own + offset, near)
        slot = gram_near.at[pass_index, near_own]
        return remote(
            slot,
            slot,
            near_send.at[pass_index, offset],
            near_recv.at[pass_index, near - offset],
            a,
            tile,
        )

    def far_copy(pass_index, offset):
        tile = near_own + near * lax.rem(far_own + offset, far)
        slot = gram_far.at[pass_index, far_own]
        return remote(
            slot,
            slot,
            far_send.at[pass_index, offset],
            far_recv.at[pass_index, far - offset],
            a,
            tile,
        )

    def sums_copy(pass_index, position, offset):
        row = lax.rem(a + offset, n_tm)
        slot = sums.at[position]
        return remote(
            slot, slot, sums_send.at[pass_index, offset], sums_recv.at[position], row, s
        )

    def start_sums(pass_index):
        value = state[pass_index]
        gram_near[pass_index, near_own] = compact(dot_exact_nt(value, value))
        for offset in range(1, near):
            near_copy(pass_index, offset).start()

    def reduce_near(pass_index):
        for offset in range(1, near):
            near_copy(pass_index, near - offset).wait_recv()
        total = gram_near[pass_index, 0]
        for slot in range(1, near):
            total = total + gram_near[pass_index, slot]
        gram_far[pass_index, far_own] = total
        for offset in range(1, far):
            far_copy(pass_index, offset).start()

    def reduce_far(pass_index, position):
        for offset in range(1, far):
            far_copy(pass_index, far - offset).wait_recv()
        total = gram_far[pass_index, 0]
        for slot in range(1, far):
            total = total + gram_far[pass_index, slot]
        sums[position, 0:COLS] = total
        for offset in range(1, n_tm):
            if pass_index == 0:
                sums_copy(0, position, offset).start()
            else:

                @pl.when(lax.rem(a + offset, n_tm) < a)
                def _():
                    sums_copy(1, position, offset).start()

    out_forward = pltpu.make_async_copy(result.at[0], forward_hbm.at[0], local_sem.at[2])
    out_adjoint = pltpu.make_async_copy(result.at[1], adjoint_hbm.at[0], local_sem.at[3])

    def combine(position, carry):
        @pl.when((position != a) & (position != last))
        def _():
            sums_copy(0, position, 1).wait_recv()

        gram = expand(sums[position, 0:COLS]) / box_total
        mix = expand(sums[position, COLS : 2 * COLS])
        size = jnp.sum(jnp.where(rows_eye == cols_eye, gram, 0.0)) / ROWS
        size = jnp.sqrt(jnp.full((8, 128), size, F32))
        size_before = size_ref[...]
        scale = scale_ref[position]
        mixed = dot_exact(mix[:, :ROWS], combined_ref[...]) / scale[0:1, :]
        squares = jnp.sum(dot_exact(mixed[:, :ROWS], gram) * mixed, axis=1, keepdims=True)
        combined = mixed / jnp.sqrt(jnp.maximum(squares, 0.0) + 1e-06)
        combined_ref[...] = combined
        size_ref[...] = size
        usable = (size > 1e-30) & (size_before > 1e-30)
        ratio = scale * (size_before / jnp.where(usable, size, 1.0))
        scale_ref[position + LAG] = jnp.where(usable, jnp.clip(ratio, 1e-12, 1e12), 1.0)

        @pl.when(position == a)
        def _():
            result[0] = dot_exact(combined[:, :ROWS], state[0])
            out_forward.start()

        @pl.when(position == last)
        def _():
            result[1] = dot_exact(combined[:, :ROWS], state[1])
            out_adjoint.start()

        return carry

    def combine_range(start, stop):
        lax.fori_loop(start, stop, combine, 0)

    def copies_source(pass_index, row, target_pass):
        value = state.at[pass_index]
        base = 4 * pass_index
        return (
            remote(
                value.at[:, pl.ds(TILE - 2 * EDGE, 2 * EDGE)],
                source_low.at[target_pass, :, pl.ds(0, 2 * EDGE)],
                source_send.at[base],
                source_recv.at[target_pass, 0],
                row,
                s + 1,
            ),
            remote(
                value.at[:, pl.ds(0, 2 * EDGE)],
                source_high.at[target_pass, :, pl.ds(EDGE, 2 * EDGE)],
                source_send.at[base + 1],
                source_recv.at[target_pass, 1],
                row,
                s - 1,
            ),
            remote(
                value.at[:, pl.ds(0, EDGE)],
                source_low.at[target_pass, :, pl.ds(2 * EDGE, EDGE)],
                source_send.at[base + 2],
                source_recv.at[target_pass, 2],
                row,
                s,
            ),
            remote(
                value.at[:, pl.ds(TILE - EDGE, EDGE)],
                source_high.at[target_pass, :, pl.ds(0, EDGE)],
                source_send.at[base + 3],
                source_recv.at[target_pass, 3],
                row,
                s,
            ),
        )

    def copy_center(pass_index, row):
        return remote(
            state.at[pass_index],
            wide.at[pass_index, :, pl.ds(EDGE, TILE)],
            wide_send.at[pass_index],
            wide_recv.at[pass_index],
            row,
            s,
        )

    def strips(pass_index, position):
        right, left, own_low, own_high = copies_source(0, a, pass_index)
        strip_right, strip_left = copies_strip(0, a, pass_index)
        scale = scale_ref[position - 1, 0:1, 0:1]
        own_low.wait_recv()
        own_high.wait_recv()

        @pl.when(has_left)
        def _():
            strip_right.wait_recv()
            high, low = halves(strip_in[pass_index, 0])
            right.wait_recv()
            wide[pass_index, :, 0:EDGE] = product(source_low[pass_index], high, low) * scale

        @pl.when(has_right)
        def _():
            strip_left.wait_recv()
            high, low = halves(strip_in[pass_index, 1])
            left.wait_recv()
            wide[pass_index, :, EDGE + TILE : 2 * EDGE + TILE] = (
                product(source_high[pass_index], high, low) * scale
            )

    def apply(pass_index, position):
        scale = scale_ref[position, 0:1, 0:1]
        for group in range(2):
            value = wide[pass_index, :, 256 * group : 256 * group + 512]
            moved = product(
                value, operator_high[pass_index, group], operator_low[pass_index, group]
            )
            state[pass_index, :, 256 * group : 256 * group + 256] = moved * scale

    adjoint_center = copy_center(1, a - 1)
    adjoint_sources = copies_source(1, a - 2, 1)

    def adjoint_position():
        strips(1, last)

        @pl.when(a < top)
        def _():
            adjoint_center.wait_recv()

        apply(1, last)

        @pl.when(a > 0)
        def _():
            adjoint_center.start()

        for copy, condition in zip(adjoint_sources, (has_right, has_left, always, always)):

            @pl.when((a > 1) & condition)
            def _():
                copy.start()

        start_sums(1)

    sent.append((a > 0, adjoint_center))
    for copy, condition in zip(adjoint_sources, (has_right, has_left, always, always)):
        sent.append(((a > 1) & condition, copy))

    send_operator()

    @pl.when(a >= top // 2)
    def _():
        prepare_adjoint()

    before_forward = jnp.maximum(a - LAG + 1, 0)
    combine_range(0, before_forward)

    @pl.when(a == 0)
    def _():
        copy_panels.wait()

    @pl.when(a < 2)
    def _():
        @pl.when(has_left)
        def _():
            state_right.wait_recv()

        @pl.when(has_right)
        def _():
            state_left.wait_recv()

    @pl.when(a >= 2)
    def _():
        strips(0, a)

    forward_center = copy_center(0, a + 1)
    receive(a > 0, forward_center)
    apply(0, a)
    send(a < top, forward_center)
    send((a == 0) & has_right, state_right)
    send((a == 0) & has_left, state_left)
    second_next = jnp.where(a < top - 1, a + 2, jnp.where(a == top - 1, top, top - 1))
    forward_sources = copies_source(0, second_next, jnp.where(a < top - 1, 0, 1))
    for copy, condition in zip(forward_sources, (has_right, has_left, always, always)):
        send(condition, copy)
    start_sums(0)

    @pl.when(a < top // 2)
    def _():
        prepare_adjoint()

    before_adjoint = jnp.maximum(last - LAG + 1, before_forward)

    @pl.when(a == top)
    def _():
        wide[1, :, EDGE : EDGE + TILE] = state[0]
        combine_range(before_forward, before_adjoint)
        adjoint_position()

    reduce_near(0)
    reduce_far(0, a)

    @pl.when(a < top)
    def _():
        combine_range(before_forward, before_adjoint)
        adjoint_position()

    reduce_near(1)
    reduce_far(1, last)
    combine_range(before_adjoint, last + 1)

    for condition, copy in sent:

        @pl.when(condition)
        def _():
            copy.wait_send()

    for pass_index in range(2):
        for offset in range(1, near):
            near_copy(pass_index, offset).wait_send()
        for offset in range(1, far):
            far_copy(pass_index, offset).wait_send()
    for offset in range(1, n_tm):
        sums_copy(0, a, offset).wait_send()

        @pl.when(lax.rem(a + offset, n_tm) < a)
        def _():
            sums_copy(1, last, offset).wait_send()

    out_forward.wait()
    out_adjoint.wait()


def solution(mesh):
    n_tm = mesh.shape["tm"]
    n_space = mesh.shape["space"]
    near = 8 if n_space >= 8 else 2
    far = n_space // near

    def shards(panels_in, blocks, block_mask, mixing):
        lines = blocks.reshape(2, TILE_BLOCKS, 3, 32, 128).transpose(0, 2, 3, 1, 4)
        lines = lines.reshape(2 * 3 * 32 * TILE_BLOCKS, 128)
        dma = pltpu.SemaphoreType.DMA
        vmem = pltpu.VMEM
        scratch = [
            vmem((2 * 3 * 32 * TILE_BLOCKS, 128), F32),
            vmem((6, TILE, 128), F32),
            vmem((4, TILE, 128), F32),
            vmem((BLOCK, 128), F32),
            vmem((BLOCK, 128), F32),
            vmem((2, BLOCK, 128), F32),
            vmem((2, BLOCK, 128), F32),
            vmem((2, 256, 512), F32),
            vmem((2, EDGE, EDGE), F32),
            vmem((2, 2, 512, 256), F32),
            vmem((2, 2, 512, 256), BF16),
            vmem((2, 2, 512, 256), BF16),
            vmem((2, 2, STRIP, EDGE), F32),
            vmem((2, ROWS, TILE + 2 * EDGE), F32),
            vmem((2, ROWS, STRIP), F32),
            vmem((2, ROWS, STRIP), F32),
            vmem((2, ROWS, TILE), F32),
            vmem((2, near, 8, 128), F32),
            vmem((2, far, 8, 128), F32),
            vmem((2 * n_tm, 2 * COLS, 128), F32),
            vmem((ROWS, 128), F32),
            vmem((8, 128), F32),
            vmem((2 * n_tm + LAG, 8, 128), F32),
            vmem((2, ROWS, TILE), F32),
            dma((4,)),
            dma((2,)),
            dma((2,)),
            dma((2,)),
            dma((2,)),
            dma((2, 2)),
            dma((2, 2)),
            dma((6,)),
            dma((4,)),
            dma((8,)),
            dma((2, 4)),
            dma((2, near)),
            dma((2, near)),
            dma((2, far)),
            dma((2, far)),
            dma((2, n_tm)),
            dma((2 * n_tm,)),
        ]
        shape = jax.ShapeDtypeStruct((1, ROWS, TILE), F32)
        return pl.pallas_call(
            functools.partial(kernel, n_tm, n_space, near),
            out_shape=(shape, shape),
            in_specs=[
                pl.BlockSpec(memory_space=pl.ANY),
                pl.BlockSpec(memory_space=pl.ANY),
                pl.BlockSpec(memory_space=pltpu.SMEM),
                pl.BlockSpec(memory_space=pltpu.VMEM),
            ],
            out_specs=(pl.BlockSpec(memory_space=pl.ANY), pl.BlockSpec(memory_space=pl.ANY)),
            scratch_shapes=scratch,
            compiler_params=pltpu.CompilerParams(collective_id=0, has_side_effects=True),
        )(panels_in, lines, block_mask.transpose(2, 0, 1), mixing)

    return jax.shard_map(
        shards,
        mesh=mesh,
        in_specs=(
            P(None, "space"),
            P("tm", "space", None, None),
            P("tm", "space", None),
            P("tm", None, None, None),
        ),
        out_specs=(P("tm", None, "space"), P("tm", None, "space")),
        check_vma=False,
    )
```
